32 devices in a mesh: row: 4 (over y, core), col: 8 (over z, x).
Axes of the slice: x: 2, y: 2, z: 4, core: 2. Of those that a mesh axis runs over, the one named last changes fastest.
Arguments:
- node_feats: bfloat16 [8192, 512], P(('row', 'col')), may hold values from -6 to 6
- w_gate: bfloat16 [512, 2048], P(None, ('row', 'col')), may hold values from -0.25 to 0.25
- w_up: bfloat16 [512, 2048], P(None, ('row', 'col')), may hold values from -0.25 to 0.25
- w_down: bfloat16 [2048, 512], P(('row', 'col')), may hold values from -0.125 to 0.125
- tile_src: int32 [512], P(('row', 'col')), may hold values from 0 to 3
- tile_dst: int32 [512], P(('row', 'col')), may hold values from 0 to 1
- tile_mask: int32 [512, 512, 512], P(('row', 'col')), may hold values 0 or 1
- tile_count: int32 [32], P(('row', 'col')), may hold values from 1 to 16, as said below
Outputs:
- entry_loss: float32 [], replicated
- grad_gate: float32 [512, 2048], P(None, ('row', 'col'))
- grad_up: float32 [512, 2048], P(None, ('row', 'col'))
- grad_down: float32 [2048, 512], P(('row', 'col'))
The draws below stay inside these ranges and needn't reach their ends.
Inputs may be any that keep to these rules, and one draw needn't show every extreme that they name: `tile_count`: some device has all 16 slots live.
All inputs are finite; a program needn't handle non-finite values. No bound on the sum of `tile_mask` on one device may be relied on, other than what follows from the above.
Results may differ from the reference program's by a relative error of at most 0.01.
Values may be sent and summed in bfloat16 or wider, within the bound.
A program may use at most 128 MiB of HBM per device.

```python
import math
import jax
import jax.numpy as jnp
import numpy as np
from jax import lax

D = 512
FF = 2048
BLOCK = 512
NODE_DEV = 256
TILE_CAP = 16
NODES = 8192
TILES = 512
SRC_BLOCKS = 4
DST_BLOCKS = 2
N_ROW = 4
N_COL = 8
DEVICES = 32


def draw_tile_count(key, part):
    counts = jax.random.randint(key, (DEVICES,), 1, TILE_CAP + 1)
    return counts.at[0].set(TILE_CAP).astype(jnp.int32)


def touch_ends(drawn, key, least, largest):
    index_at = [jax.random.randint(jax.random.fold_in(key, axis), (), 0, length) for axis, length in enumerate(drawn.shape)]
    main_axis = drawn.shape.index(max(drawn.shape))
    neighbour = index_at[:main_axis] + [(index_at[main_axis] + 1) % drawn.shape[main_axis]] + index_at[main_axis + 1:]
    return drawn.at[tuple(index_at)].set(least).at[tuple(neighbour)].set(largest)


def levels(own_key, shape, pieces, smallest, largest):
    gain = 1.0
    for position, parts in pieces:
        draws = jax.random.uniform(jax.random.fold_in(jax.random.fold_in(own_key, 6), position), (parts,), jnp.float32, smallest / len(pieces), largest / len(pieces))
        gain = gain * jnp.repeat(jnp.exp(draws), shape[position] // parts).reshape((-1,) + (1,) * (len(shape) - 1 - position))
    return gain


def rank_table(amount, skew):
    weights = [(1 << 20) // math.isqrt(grade ** skew) + 1 for grade in range(1, amount + 1)]
    spread = 1 + sum(weights) // (1 << 30)
    return np.cumsum(np.array([max(1, weight // spread) for weight in weights]))


def ranked_ids(key, extent, number_of, slope):
    table = rank_table(number_of, slope)
    ticket = jax.random.randint(jax.random.fold_in(key, 1), extent, 0, int(table[number_of - 1]))
    grade = jnp.searchsorted(jnp.asarray(table, jnp.int32), ticket, side="right")
    return jax.random.permutation(jax.random.fold_in(key, 2), number_of)[grade].astype(jnp.int32)


def noise(stream_key, extent, scale, most, shards=(), held_as=jnp.bfloat16):
    loudness = levels(stream_key, extent, shards, -0.22, 0.18) if shards else 1.0
    array = jax.random.normal(stream_key, extent, jnp.float32) * scale * loudness
    return jnp.minimum(jnp.maximum(array, -most), most).astype(held_as)


def setup_inputs(seed: int = 0) -> dict:
    key_of = jax.random.split(jax.random.key(seed), 9)
    return {
        "node_feats": noise(key_of[0], (NODES, D), 1.0, 6.0, ((0, 32),)),
        "w_gate": noise(key_of[1], (D, FF), D ** -0.5, 0.25, ((1, 32),)),
        "w_up": noise(key_of[2], (D, FF), D ** -0.5, 0.25, ((1, 32),)),
        "w_down": noise(key_of[3], (FF, D), FF ** -0.5, 0.125, ((0, 32),)),
        "tile_src": touch_ends(ranked_ids(key_of[4], (TILES,), SRC_BLOCKS, 2), jax.random.fold_in(key_of[4], 3), 0, SRC_BLOCKS - 1).astype(jnp.int32),
        "tile_dst": touch_ends(ranked_ids(key_of[5], (TILES,), DST_BLOCKS, 1), jax.random.fold_in(key_of[5], 3), 0, DST_BLOCKS - 1).astype(jnp.int32),
        "tile_mask": touch_ends((jax.random.randint(key_of[6], (TILES, BLOCK, BLOCK), 0, 8) < 1).astype(jnp.int32), jax.random.fold_in(key_of[6], 1), 0, 1),
        "tile_count": draw_tile_count(jax.random.fold_in(key_of[8], 71), 0),
    }


def reference(node_feats, w_gate, w_up, w_down, tile_src, tile_dst, tile_mask, tile_count):
    gate_proj = jnp.dot(node_feats, w_gate, preferred_element_type=jnp.float32)
    up_proj = jnp.dot(node_feats, w_up, preferred_element_type=jnp.float32)
    hidden = (jax.nn.silu(gate_proj) * up_proj).astype(jnp.bfloat16)
    embedding = (node_feats.astype(jnp.float32) + jnp.dot(hidden, w_down, preferred_element_type=jnp.float32)).astype(jnp.bfloat16)
    across = embedding.reshape(N_ROW, N_COL, NODE_DEV, D).transpose(1, 0, 2, 3).reshape(NODES, D)
    tiles_live = jnp.sum(tile_count).astype(jnp.float32)
    score_scale = D ** -0.5
    grad_factor = score_scale / tiles_live
    src_span = N_COL * NODE_DEV
    dst_span = N_ROW * NODE_DEV

    def device_step(carry, device):
        loss_sum, src_accum, dst_accum = carry
        row_index = device // N_COL
        col_index = device % N_COL
        src_rows = lax.dynamic_slice_in_dim(embedding, (row_index * src_span).astype(jnp.int32), src_span, 0)
        dst_rows = lax.dynamic_slice_in_dim(across, (col_index * dst_span).astype(jnp.int32), dst_span, 0)
        live_slots = tile_count[device]

        def slot_step(inner, slot):
            loss_part, src_part, dst_part = inner
            tile_id = (device * TILE_CAP + slot).astype(jnp.int32)
            live = (slot < live_slots).astype(jnp.float32)
            src_start = (tile_src[tile_id] * BLOCK).astype(jnp.int32)
            dst_start = (tile_dst[tile_id] * BLOCK).astype(jnp.int32)
            src_block = lax.dynamic_slice_in_dim(src_rows, src_start, BLOCK, 0)
            dst_block = lax.dynamic_slice_in_dim(dst_rows, dst_start, BLOCK, 0)
            scores = lax.dot_general(src_block, dst_block, (((1,), (1,)), ((), ())), preferred_element_type=jnp.float32) * score_scale
            labels = lax.dynamic_index_in_dim(tile_mask, tile_id, 0, keepdims=False).astype(jnp.float32)
            loss_part = loss_part + live * jnp.sum(jax.nn.softplus(scores) - labels * scores)
            score_grad = ((jax.nn.sigmoid(scores) - labels) * grad_factor).astype(jnp.bfloat16)
            src_term = jnp.dot(score_grad, dst_block, preferred_element_type=jnp.float32) * live
            dst_term = lax.dot_general(score_grad, src_block, (((0,), (0,)), ((), ())), preferred_element_type=jnp.float32) * live
            old_src = lax.dynamic_slice_in_dim(src_part, src_start, BLOCK, 0)
            src_part = lax.dynamic_update_slice_in_dim(src_part, old_src + src_term, src_start, 0)
            old_dst = lax.dynamic_slice_in_dim(dst_part, dst_start, BLOCK, 0)
            dst_part = lax.dynamic_update_slice_in_dim(dst_part, old_dst + dst_term, dst_start, 0)
            return (loss_part, src_part, dst_part), None

        start_inner = (jnp.zeros((), jnp.float32), jnp.zeros((src_span, D), jnp.float32), jnp.zeros((dst_span, D), jnp.float32))
        (loss_part, src_part, dst_part), unused = lax.scan(slot_step, start_inner, jnp.arange(TILE_CAP, dtype=jnp.int32))
        src_round = lax.optimization_barrier(src_part.astype(jnp.bfloat16)).astype(jnp.float32)
        dst_round = lax.optimization_barrier(dst_part.astype(jnp.bfloat16)).astype(jnp.float32)
        src_begin = (row_index * src_span).astype(jnp.int32)
        dst_begin = (col_index * dst_span).astype(jnp.int32)
        src_accum = lax.dynamic_update_slice_in_dim(src_accum, lax.dynamic_slice_in_dim(src_accum, src_begin, src_span, 0) + src_round, src_begin, 0)
        dst_accum = lax.dynamic_update_slice_in_dim(dst_accum, lax.dynamic_slice_in_dim(dst_accum, dst_begin, dst_span, 0) + dst_round, dst_begin, 0)
        return (loss_sum + loss_part, src_accum, dst_accum), None

    start_outer = (jnp.zeros((), jnp.float32), jnp.zeros((NODES, D), jnp.float32), jnp.zeros((NODES, D), jnp.float32))
    (loss_sum, src_accum, dst_accum), unused = lax.scan(device_step, start_outer, jnp.arange(N_ROW * N_COL, dtype=jnp.int32))
    dst_back = dst_accum.reshape(N_COL, N_ROW, NODE_DEV, D).transpose(1, 0, 2, 3).reshape(NODES, D)
    embed_grad = (src_accum + dst_back).astype(jnp.bfloat16)
    entry_loss = loss_sum / (tiles_live * BLOCK * BLOCK)
    grad_down = lax.dot_general(hidden, embed_grad, (((0,), (0,)), ((), ())), preferred_element_type=jnp.float32)
    hidden_grad = lax.dot_general(embed_grad, w_down, (((1,), (1,)), ((), ())), preferred_element_type=jnp.float32)
    sig = jax.nn.sigmoid(gate_proj)
    gate_grad = (hidden_grad * up_proj * sig * (1.0 + gate_proj * (1.0 - sig))).astype(jnp.bfloat16)
    up_grad = (hidden_grad * gate_proj * sig).astype(jnp.bfloat16)
    grad_gate = lax.dot_general(node_feats, gate_grad, (((0,), (0,)), ((), ())), preferred_element_type=jnp.float32)
    grad_up = lax.dot_general(node_feats, up_grad, (((0,), (0,)), ((), ())), preferred_element_type=jnp.float32)
    return (entry_loss, grad_gate, grad_up, grad_down)
```

```python
import functools
import math

import jax
import jax.numpy as jnp
from jax import lax
from jax.experimental import pallas as pl
from jax.experimental.pallas import tpu as pltpu
from jax.sharding import PartitionSpec as P

BLOCK = 512
F32 = jnp.float32
BF16 = jnp.bfloat16
NT = (((1,), (1,)), ((), ()))
TN = (((0,), (0,)), ((), ()))


def dot_nt(a, b):
    return lax.dot_general(a, b, NT, preferred_element_type=F32)


def dot_tn(a, b):
    return lax.dot_general(a, b, TN, preferred_element_type=F32)


def halve(x, op, rows):
    while x.shape[0] > rows:
        half = x.shape[0] // 2
        x = op(x[:half], x[half:])
    return x


def tile_kernel(half_scale, count_ref, src_id, dst_id, src_ref, dst_ref, mask_ref,
                src_out, dst_out, loss_out, src_acc, dst_acc, grad_buf, hinge_acc, log_acc):
    slot = pl.program_id(0)
    width = src_ref.shape[1]

    @pl.when(slot == 0)
    def _():
        src_acc[...] = jnp.zeros_like(src_acc)
        dst_acc[...] = jnp.zeros_like(dst_acc)
        hinge_acc[...] = jnp.zeros_like(hinge_acc)
        log_acc[...] = jnp.zeros_like(log_acc)

    @pl.when(slot < count_ref[0])
    def _():
        src_at = pl.ds(pl.multiple_of(src_id[slot] * BLOCK, BLOCK), BLOCK)
        dst_at = pl.ds(pl.multiple_of(dst_id[slot] * BLOCK, BLOCK), BLOCK)
        dst_block = dst_ref[dst_at, :]
        prods = None
        part = 128
        for lo in range(0, BLOCK, part):
            rows = pl.ds(pl.multiple_of(src_id[slot] * BLOCK + lo, part), part)
            raw = dot_nt(src_ref[rows, :], dst_block)
            sign = jnp.where(mask_ref[0, lo:lo + part, :] == 0, 1.0, -1.0)
            half = jnp.tanh(raw * half_scale)
            grad_buf[lo:lo + part, :] = (half + sign).astype(BF16)
            hinge_acc[...] += halve(jnp.maximum(raw * sign, 0.0), jnp.add, 8)
            prod = halve(1.0 + jnp.abs(half), jnp.multiply, 8)
            prods = prod if prods is None else prods * prod
        log_acc[...] += (BLOCK // 8) * math.log(2.0) - jnp.log(prods)
        grad = grad_buf[...]
        src_acc[src_at, :] += jnp.dot(grad, dst_block, preferred_element_type=F32)
        dst_acc[dst_at, :] += dot_tn(grad, src_ref[src_at, :])

    @pl.when(slot == pl.num_programs(0) - 1)
    def _():
        src_out[...] = src_acc[...].astype(BF16)
        dst_out[...] = dst_acc[...].astype(BF16)
        total = hinge_acc[...] * (2.0 * half_scale) + log_acc[...]
        loss_out[...] = jnp.broadcast_to(jnp.sum(total, keepdims=True), loss_out.shape)


def tiles(src_rows, dst_rows, tile_src, tile_dst, tile_mask, tile_count):
    slots = tile_mask.shape[0]
    width = src_rows.shape[1]
    whole = lambda j, *_: (0, 0)
    return pl.pallas_call(
        functools.partial(tile_kernel, 0.5 * width ** -0.5),
        out_shape=(
            jax.ShapeDtypeStruct(src_rows.shape, BF16),
            jax.ShapeDtypeStruct(dst_rows.shape, BF16),
            jax.ShapeDtypeStruct((8, 128), F32),
        ),
        grid_spec=pltpu.PrefetchScalarGridSpec(
            num_scalar_prefetch=3,
            grid=(slots,),
            in_specs=[
                pl.BlockSpec(src_rows.shape, whole, pipeline_mode=pl.Buffered(1)),
                pl.BlockSpec(dst_rows.shape, whole, pipeline_mode=pl.Buffered(1)),
                pl.BlockSpec((1, BLOCK, BLOCK), lambda j, n, s, d: (jnp.minimum(j, n[0] - 1), 0, 0)),
            ],
            out_specs=[
                pl.BlockSpec(src_rows.shape, whole, pipeline_mode=pl.Buffered(1)),
                pl.BlockSpec(dst_rows.shape, whole, pipeline_mode=pl.Buffered(1)),
                pl.BlockSpec((8, 128), whole),
            ],
            scratch_shapes=[
                pltpu.VMEM(src_rows.shape, F32),
                pltpu.VMEM(dst_rows.shape, F32),
                pltpu.VMEM((BLOCK, BLOCK), BF16),
                pltpu.VMEM((8, BLOCK), F32),
                pltpu.VMEM((8, BLOCK), F32),
            ],
        ),
        compiler_params=pltpu.CompilerParams(vmem_limit_bytes=48 << 20),
        name="tiles",
    )(tile_count, tile_src, tile_dst, src_rows, dst_rows, tile_mask)


def per_device(node_feats, w_gate, w_up, w_down, tile_src, tile_dst, tile_mask, tile_count):
    width = node_feats.shape[1]
    stacked = jnp.stack((w_gate.T, w_up.T, w_down))
    weights = lax.all_gather(stacked, "col", axis=1, tiled=True)
    feats = lax.all_gather(node_feats, "row", axis=0, tiled=True)
    gate_proj = dot_nt(feats, weights[0])
    up_proj = dot_nt(feats, weights[1])
    hidden = (jax.nn.silu(gate_proj) * up_proj).astype(BF16)
    branch = jnp.dot(hidden, weights[2], preferred_element_type=F32).astype(BF16)
    branch_out = lax.psum_scatter(branch, "row", scatter_dimension=0, tiled=True)
    embedding = (node_feats.astype(F32) + branch_out.astype(F32)).astype(BF16)
    src_rows = lax.all_gather(embedding, "col", axis=0, tiled=True)
    dst_rows = lax.all_gather(embedding, "row", axis=0, tiled=True)
    src_part, dst_part, loss_part = tiles(src_rows, dst_rows, tile_src, tile_dst, tile_mask, tile_count)
    src_grad = lax.psum_scatter(src_part, "col", scatter_dimension=0, tiled=True)
    dst_grad = lax.psum_scatter(dst_part, "row", scatter_dimension=0, tiled=True)
    own_grad = (src_grad.astype(F32) + dst_grad.astype(F32)).astype(BF16)
    totals = lax.psum(jnp.stack((loss_part[0, 0], tile_count[0].astype(F32))), ("row", "col"))
    embed_grad = lax.all_gather(own_grad, "row", axis=0, tiled=True)
    hidden_grad = dot_nt(embed_grad, weights[2])
    sig = jax.nn.sigmoid(gate_proj)
    gate_grad = (hidden_grad * up_proj * sig * (1.0 + gate_proj * (1.0 - sig))).astype(BF16)
    up_grad = (hidden_grad * gate_proj * sig).astype(BF16)
    partial = jnp.stack(
        (dot_tn(gate_grad, feats).astype(BF16), dot_tn(up_grad, feats).astype(BF16), dot_tn(hidden, embed_grad).astype(BF16))
    )
    summed = lax.psum_scatter(partial, "col", scatter_dimension=1, tiled=True).astype(F32)
    summed = summed * (0.5 * width ** -0.5 / totals[1])
    entry_loss = totals[0] / (totals[1] * BLOCK * BLOCK)
    return (entry_loss, summed[0].T, summed[1].T, summed[2])


def solution(mesh):
    both = ("row", "col")
    in_specs = (
        P(both, None),
        P(None, both),
        P(None, both),
        P(both, None),
        P(both),
        P(both),
        P(both, None, None),
        P(both),
    )
    out_specs = (P(), P(None, both), P(None, both), P(both, None))
    return jax.shard_map(per_device, mesh=mesh, in_specs=in_specs, out_specs=out_specs, check_vma=False)
```

```python
import functools
import math

import jax
import jax.numpy as jnp
from jax import lax
from jax.experimental import pallas as pl
from jax.experimental.pallas import tpu as pltpu
from jax.sharding import PartitionSpec as P

BLOCK = 512
F32 = jnp.float32
BF16 = jnp.bfloat16
NT = (((1,), (1,)), ((), ()))
TN = (((0,), (0,)), ((), ()))


def dot_nt(a, b):
    return lax.dot_general(a, b, NT, preferred_element_type=F32)


def dot_tn(a, b):
    return lax.dot_general(a, b, TN, preferred_element_type=F32)


def halve(x, op, rows):
    while x.shape[0] > rows:
        half = x.shape[0] // 2
        x = op(x[:half], x[half:])
    return x


def tile_kernel(half_scale, count_ref, src_id, dst_id, src_ref, dst_ref, mask_ref,
                src_out, dst_out, loss_out, src_acc, dst_acc, grad_buf, hinge_acc, log_acc):
    slot = pl.program_id(0)
    width = src_ref.shape[1]

    @pl.when(slot == 0)
    def _():
        src_acc[...] = jnp.zeros_like(src_acc)
        dst_acc[...] = jnp.zeros_like(dst_acc)
        hinge_acc[...] = jnp.zeros_like(hinge_acc)
        log_acc[...] = jnp.zeros_like(log_acc)

    @pl.when(slot < count_ref[0])
    def _():
        src_at = pl.ds(pl.multiple_of(src_id[slot] * BLOCK, BLOCK), BLOCK)
        dst_at = pl.ds(pl.multiple_of(dst_id[slot] * BLOCK, BLOCK), BLOCK)
        dst_block = dst_ref[dst_at, :]
        prods = None
        part = 128
        for lo in range(0, BLOCK, part):
            rows = pl.ds(pl.multiple_of(src_id[slot] * BLOCK + lo, part), part)
            raw = dot_nt(src_ref[rows, :], dst_block)
            sign = jnp.where(mask_ref[0, lo:lo + part, :] == 0, 1.0, -1.0)
            half = jnp.tanh(raw * half_scale)
            grad_buf[lo:lo + part, :] = (half + sign).astype(BF16)
            hinge_acc[...] += halve(jnp.maximum(raw * sign, 0.0), jnp.add, 8)
            prod = halve(1.0 + jnp.abs(half), jnp.multiply, 8)
            prods = prod if prods is None else prods * prod
        log_acc[...] += (BLOCK // 8) * math.log(2.0) - jnp.log(prods)
        grad = grad_buf[...]
        src_acc[src_at, :] += jnp.dot(grad, dst_block, preferred_element_type=F32)
        dst_acc[dst_at, :] += dot_tn(grad, src_ref[src_at, :])

    @pl.when(slot == pl.num_programs(0) - 1)
    def _():
        src_out[...] = src_acc[...].astype(BF16)
        dst_out[...] = dst_acc[...].astype(BF16)
        total = hinge_acc[...] * (2.0 * half_scale) + log_acc[...]
        loss_out[...] = jnp.broadcast_to(jnp.sum(total, keepdims=True), loss_out.shape)


def tiles(src_rows, dst_rows, tile_src, tile_dst, tile_mask, tile_count):
    slots = tile_mask.shape[0]
    width = src_rows.shape[1]
    whole = lambda j, *_: (0, 0)
    return pl.pallas_call(
        functools.partial(tile_kernel, 0.5 * width ** -0.5),
        out_shape=(
            jax.ShapeDtypeStruct(src_rows.shape, BF16),
            jax.ShapeDtypeStruct(dst_rows.shape, BF16),
            jax.ShapeDtypeStruct((8, 128), F32),
        ),
        grid_spec=pltpu.PrefetchScalarGridSpec(
            num_scalar_prefetch=3,
            grid=(slots,),
            in_specs=[
                pl.BlockSpec(src_rows.shape, whole, pipeline_mode=pl.Buffered(1)),
                pl.BlockSpec(dst_rows.shape, whole, pipeline_mode=pl.Buffered(1)),
                pl.BlockSpec((1, BLOCK, BLOCK), lambda j, n, s, d: (jnp.minimum(j, n[0] - 1), 0, 0)),
            ],
            out_specs=[
                pl.BlockSpec(src_rows.shape, whole, pipeline_mode=pl.Buffered(1)),
                pl.BlockSpec(dst_rows.shape, whole, pipeline_mode=pl.Buffered(1)),
                pl.BlockSpec((8, 128), whole),
            ],
            scratch_shapes=[
                pltpu.VMEM(src_rows.shape, F32),
                pltpu.VMEM(dst_rows.shape, F32),
                pltpu.VMEM((BLOCK, BLOCK), BF16),
                pltpu.VMEM((8, BLOCK), F32),
                pltpu.VMEM((8, BLOCK), F32),
            ],
        ),
        compiler_params=pltpu.CompilerParams(vmem_limit_bytes=48 << 20),
        name="tiles",
    )(tile_count, tile_src, tile_dst, src_rows, dst_rows, tile_mask)


def finish(steps):
    steps = list(steps)
    while steps:
        steps = [step for step in steps if next(step, True) is None]


def group(axis, n, inner):
    me = lax.axis_index(axis)
    return me, me // inner, lax.rem(me, inner)


def gather(axis, n, inner, src, place, send, recv):
    outer = n // inner
    me, at_o, at_i = group(axis, n, inner)

    def line(way, k):
        block = at_o - k if way == 0 else at_o + k
        ahead = me + inner if way == 0 else me - inner
        index = way * (outer - 1) + k
        return pltpu.make_async_remote_copy(
            src_ref=src if k == 0 else place(block * inner + at_i),
            dst_ref=place(me if k == 0 else block * inner + at_i),
            send_sem=send.at[index],
            recv_sem=recv.at[index],
            device_id={axis: ahead},
        )

    def sends(way, k):
        if way == 0:
            return jnp.logical_and(at_o - k >= 0, at_o < outer - 1)
        return jnp.logical_and(at_o + k < outer, at_o > 0)

    def arrived(way, k):
        block = at_o - 1 - k if way == 0 else at_o + 1 + k
        index = way * (outer - 1) + k
        here = place(block * inner + at_i)
        return pltpu.make_async_remote_copy(
            src_ref=here, dst_ref=here, send_sem=send.at[index], recv_sem=recv.at[index], device_id={axis: me}
        )

    def arrives(way, k):
        return at_o - 1 - k >= 0 if way == 0 else at_o + 1 + k < outer

    def across(j, block, slot, own, incoming=False):
        index = 2 * (outer - 1) + (j - 1) * (2 * outer - 1) + slot
        peer = at_o * inner + lax.rem(at_i + j, inner)
        where = place(block * inner + (lax.rem(at_i + inner - j, inner) if incoming else at_i))
        return pltpu.make_async_remote_copy(
            src_ref=src if own else where,
            dst_ref=where,
            send_sem=send.at[index],
            recv_sem=recv.at[index],
            device_id={axis: peer},
        )

    def slots():
        for way in range(2):
            for k in range(outer - 1):
                yield way, k, (at_o - 1 - k if way == 0 else at_o + 1 + k), 1 + way * (outer - 1) + k

    for way in range(2):
        @pl.when(sends(way, 0))
        def _(way=way):
            line(way, 0).start()
    for j in range(1, inner):
        across(j, at_o, 0, True).start()
    here = place(me)
    here[...] = src[...]
    yield
    for step in range(outer - 1):
        for way, k, block, slot in slots():
            if k != step:
                continue

            @pl.when(arrives(way, k))
            def _(way=way, k=k, block=block, slot=slot):
                arrived(way, k).wait_recv()
                for j in range(1, inner):
                    across(j, block, slot, False).start()
                if k + 1 < outer - 1:
                    @pl.when(sends(way, k + 1))
                    def _():
                        line(way, k + 1).start()
        yield
    for j in range(1, inner):
        across(j, at_o, 0, True, True).wait_recv()
        across(j, at_o, 0, True).wait_send()
    for way, k, block, slot in slots():
        @pl.when(arrives(way, k))
        def _(block=block, slot=slot):
            for j in range(1, inner):
                across(j, block, slot, False, True).wait_recv()
                across(j, block, slot, False).wait_send()

        @pl.when(sends(way, k))
        def _(way=way, k=k):
            line(way, k).wait_send()


def gather_sems(n, inner):
    outer = n // inner
    count = 2 * (outer - 1) + (inner - 1) * (2 * outer - 1)
    return [pltpu.SemaphoreType.DMA((count,)), pltpu.SemaphoreType.DMA((count,))]


def reduce(axis, n, inner, place, near, out, far, send, recv, result):
    outer = n // inner
    me, at_o, at_i = group(axis, n, inner)
    order = sorted(range(outer), key=lambda off: -min(off, outer - off))

    def across(j, off):
        index = (j - 1) * outer + off
        block = lax.rem(at_o + off, outer) * inner + lax.rem(at_i + j, inner)
        return pltpu.make_async_remote_copy(
            src_ref=place(block),
            dst_ref=near.at[index],
            send_sem=send.at[index],
            recv_sem=recv.at[index],
            device_id={axis: at_o * inner + lax.rem(at_i + j, inner)},
        )

    def along(off):
        index = (inner - 1) * outer + off - 1
        return pltpu.make_async_remote_copy(
            src_ref=out.at[off - 1],
            dst_ref=far.at[off - 1],
            send_sem=send.at[index],
            recv_sem=recv.at[index],
            device_id={axis: lax.rem(at_o + off, outer) * inner + at_i},
        )

    for off in order:
        for j in range(1, inner):
            across(j, off).start()
    yield
    for off in order:
        total = place(lax.rem(at_o + off, outer) * inner + at_i)[...].astype(F32)
        for j in range(1, inner):
            across(j, off).wait_recv()
            total = total + near[(j - 1) * outer + off].astype(F32)
        if off:
            out[off - 1] = total.astype(BF16)
            along(off).start()
            yield
    for off in order[:-1]:
        along(off).wait_recv()
        total = total + far[off - 1].astype(F32)
    result.append(total)
    for off in order:
        for j in range(1, inner):
            across(j, off).wait_send()
        if off:
            along(off).wait_send()


def reduce_scratch(n, inner, block):
    outer = n // inner
    count = (inner - 1) * outer + outer - 1
    return [
        pltpu.VMEM(((inner - 1) * outer,) + block, BF16),
        pltpu.VMEM((outer - 1,) + block, BF16),
        pltpu.VMEM((outer - 1,) + block, BF16),
        pltpu.SemaphoreType.DMA((count,)),
        pltpu.SemaphoreType.DMA((count,)),
    ]


def sum_over(axis, n, src, slots, send, recv, result):
    me = lax.axis_index(axis)

    def copy(j):
        return pltpu.make_async_remote_copy(
            src_ref=src,
            dst_ref=slots.at[j - 1],
            send_sem=send.at[j - 1],
            recv_sem=recv.at[j - 1],
            device_id={axis: lax.rem(me + j, n)},
        )

    for j in range(1, n):
        copy(j).start()
    yield
    total = src[...]
    for j in range(1, n):
        copy(j).wait_recv()
        total = total + slots[j - 1]
    result.append(total)
    for j in range(1, n):
        copy(j).wait_send()


def sum_scratch(n):
    return [
        pltpu.VMEM((n - 1, 8, 128), F32),
        pltpu.SemaphoreType.DMA((n - 1,)),
        pltpu.SemaphoreType.DMA((n - 1,)),
    ]


def greet(axes):
    barrier = pltpu.get_barrier_semaphore()
    total = 0
    for axis, n in axes:
        me = lax.axis_index(axis)
        for j in range(1, n):
            pl.semaphore_signal(barrier, inc=1, device_id={axis: lax.rem(me + j, n)})
        total += n - 1
    pl.semaphore_wait(barrier, total)


def rows_of(ref, size):
    return lambda block: ref.at[pl.ds(pl.multiple_of(block * size, size), size), :]


def units_of(ref, size):
    return lambda block: ref.at[:, pl.ds(pl.multiple_of(block * size, size), size), :]


def gather_in_kernel(row, col, w_ref, x_ref, w_out, x_out, *sems):
    greet((("row", row[0]), ("col", col[0])))
    finish((
        gather("col", *col, w_ref, units_of(w_out, w_ref.shape[1]), *sems[:2]),
        gather("row", *row, x_ref, rows_of(x_out, x_ref.shape[0]), *sems[2:]),
    ))


def embed_kernel(row, col, branch_ref, x_ref, src_out, dst_out, held, *scratch):
    greet((("row", row[0]), ("col", col[0])))
    size = x_ref.shape[0]
    branch = []
    finish((reduce("row", *row, rows_of(branch_ref, size), *scratch[:5], branch),))
    held[...] = (x_ref[...].astype(F32) + branch[0]).astype(BF16)
    finish((
        gather("col", *col, held, rows_of(src_out, size), *scratch[5:7]),
        gather("row", *row, held, rows_of(dst_out, size), *scratch[7:9]),
    ))


def grad_kernel(row, col, src_ref, dst_ref, tot_ref, grad_out, tot_out, held, tot_held, *scratch):
    greet((("row", row[0]), ("col", col[0])))
    size = held.shape[0]
    own, first, second = [], [], []

    def totals():
        yield from sum_over("row", row[0], tot_ref, *scratch[12:15], first)
        tot_held[...] = first[0]
        yield
        yield from sum_over("col", col[0], tot_held, *scratch[15:18], second)
        tot_out[...] = second[0]

    finish((
        reduce("col", *col, rows_of(src_ref, size), *scratch[:5], own),
        reduce("row", *row, rows_of(dst_ref, size), *scratch[5:10], own),
        totals(),
    ))
    held[...] = (own[0] + own[1]).astype(BF16)
    finish((gather("row", *row, held, rows_of(grad_out, size), *scratch[10:12]),))


def weight_kernel(col, part_ref, sum_out, *scratch):
    greet((("col", col[0]),))
    total = []
    finish((reduce("col", *col, units_of(part_ref, sum_out.shape[1]), *scratch, total),))
    sum_out[...] = total[0]


def remote(kernel, name, number, outs, scratch):
    vmem = pl.BlockSpec(memory_space=pltpu.VMEM)
    return pl.pallas_call(
        kernel,
        out_shape=outs,
        out_specs=jax.tree.map(lambda _: vmem, outs),
        scratch_shapes=scratch,
        compiler_params=pltpu.CompilerParams(
            collective_id=number, has_side_effects=True, vmem_limit_bytes=32 << 20
        ),
        name=name,
    )


def per_device(row, col, node_feats, w_gate, w_up, w_down, tile_src, tile_dst, tile_mask, tile_count):
    size, width = node_feats.shape
    units = w_down.shape[0]
    shaped = jax.ShapeDtypeStruct
    src_shape = shaped((col[0] * size, width), BF16)
    dst_shape = shaped((row[0] * size, width), BF16)
    stacked = jnp.stack((w_gate.T, w_up.T, w_down))
    weights, feats = remote(
        functools.partial(gather_in_kernel, row, col),
        "gather_in",
        0,
        (shaped((3, col[0] * units, width), BF16), dst_shape),
        gather_sems(*col) + gather_sems(*row),
    )(stacked, node_feats)
    gate_proj = dot_nt(feats, weights[0])
    up_proj = dot_nt(feats, weights[1])
    hidden = (jax.nn.silu(gate_proj) * up_proj).astype(BF16)
    branch = jnp.dot(hidden, weights[2], preferred_element_type=F32).astype(BF16)
    src_rows, dst_rows = remote(
        functools.partial(embed_kernel, row, col),
        "embed",
        1,
        (src_shape, dst_shape),
        [pltpu.VMEM((size, width), BF16)]
        + reduce_scratch(*row, (size, width)) + gather_sems(*col) + gather_sems(*row),
    )(branch, node_feats)
    src_part, dst_part, loss_part = tiles(src_rows, dst_rows, tile_src, tile_dst, tile_mask, tile_count)
    is_loss = lax.broadcasted_iota(jnp.int32, loss_part.shape, 0) == 0
    embed_grad, totals = remote(
        functools.partial(grad_kernel, row, col),
        "grad",
        2,
        (dst_shape, shaped(loss_part.shape, F32)),
        [pltpu.VMEM((size, width), BF16), pltpu.VMEM(loss_part.shape, F32)]
        + reduce_scratch(*col, (size, width)) + reduce_scratch(*row, (size, width)) + gather_sems(*row)
        + sum_scratch(row[0]) + sum_scratch(col[0]),
    )(src_part, dst_part, jnp.where(is_loss, loss_part, tile_count[0].astype(F32)))
    hidden_grad = dot_nt(embed_grad, weights[2])
    sig = jax.nn.sigmoid(gate_proj)
    gate_grad = (hidden_grad * up_proj * sig * (1.0 + gate_proj * (1.0 - sig))).astype(BF16)
    up_grad = (hidden_grad * gate_proj * sig).astype(BF16)
    partial = jnp.stack(
        (dot_tn(gate_grad, feats).astype(BF16), dot_tn(up_grad, feats).astype(BF16), dot_tn(hidden, embed_grad).astype(BF16))
    )
    summed = remote(
        functools.partial(weight_kernel, col),
        "weight",
        3,
        shaped((3, units, width), F32),
        reduce_scratch(*col, (3, units, width)),
    )(partial)
    summed = summed * (0.5 * width ** -0.5 / totals[1, 0])
    entry_loss = totals[0, 0] / (totals[1, 0] * BLOCK * BLOCK)
    return (entry_loss, summed[0].T, summed[1].T, summed[2])


def solution(mesh):
    both = ("row", "col")
    in_specs = (
        P(both, None),
        P(None, both),
        P(None, both),
        P(both, None),
        P(both),
        P(both),
        P(both, None, None),
        P(both),
    )
    out_specs = (P(), P(None, both), P(None, both), P(both, None))
    row = (mesh.shape["row"], 2)
    col = (mesh.shape["col"], mesh.shape["col"] // 4)
    return jax.shard_map(functools.partial(per_device, row, col), mesh=mesh, in_specs=in_specs, out_specs=out_specs, check_vma=False)
```

```python
import functools
import math

import jax
import jax.numpy as jnp
from jax import lax
from jax.experimental import pallas as pl
from jax.experimental.pallas import tpu as pltpu
from jax.sharding import PartitionSpec as P

BLOCK = 512
CHUNKS = 4
F32 = jnp.float32
BF16 = jnp.bfloat16
NT = (((1,), (1,)), ((), ()))
TN = (((0,), (0,)), ((), ()))


def dot_nt(a, b):
    return lax.dot_general(a, b, NT, preferred_element_type=F32)


def dot_tn(a, b):
    return lax.dot_general(a, b, TN, preferred_element_type=F32)


def halve(x, op, rows):
    while x.shape[0] > rows:
        half = x.shape[0] // 2
        x = op(x[:half], x[half:])
    return x


def tile_kernel(half_scale, count_ref, src_id, dst_id, src_ref, dst_ref, mask_ref,
                src_out, dst_out, loss_out, src_acc, dst_acc, grad_buf, hinge_acc, log_acc):
    slot = pl.program_id(0)
    width = src_ref.shape[1]

    @pl.when(slot == 0)
    def _():
        src_acc[...] = jnp.zeros_like(src_acc)
        dst_acc[...] = jnp.zeros_like(dst_acc)
        hinge_acc[...] = jnp.zeros_like(hinge_acc)
        log_acc[...] = jnp.zeros_like(log_acc)

    @pl.when(slot < count_ref[0])
    def _():
        src_at = pl.ds(pl.multiple_of(src_id[slot] * BLOCK, BLOCK), BLOCK)
        dst_at = pl.ds(pl.multiple_of(dst_id[slot] * BLOCK, BLOCK), BLOCK)
        dst_block = dst_ref[dst_at, :]
        prods = None
        part = 128
        for lo in range(0, BLOCK, part):
            rows = pl.ds(pl.multiple_of(src_id[slot] * BLOCK + lo, part), part)
            raw = dot_nt(src_ref[rows, :], dst_block)
            sign = jnp.where(mask_ref[0, lo:lo + part, :] == 0, 1.0, -1.0)
            half = jnp.tanh(raw * half_scale)
            grad_buf[lo:lo + part, :] = (half + sign).astype(BF16)
            hinge_acc[...] += halve(jnp.maximum(raw * sign, 0.0), jnp.add, 8)
            prod = halve(1.0 + jnp.abs(half), jnp.multiply, 8)
            prods = prod if prods is None else prods * prod
        log_acc[...] += (BLOCK // 8) * math.log(2.0) - jnp.log(prods)
        grad = grad_buf[...]
        src_acc[src_at, :] += jnp.dot(grad, dst_block, preferred_element_type=F32)
        dst_acc[dst_at, :] += dot_tn(grad, src_ref[src_at, :])

    @pl.when(slot == pl.num_programs(0) - 1)
    def _():
        src_out[...] = src_acc[...].astype(BF16)
        dst_out[...] = dst_acc[...].astype(BF16)
        total = hinge_acc[...] * (2.0 * half_scale) + log_acc[...]
        loss_out[...] = jnp.broadcast_to(jnp.sum(total, keepdims=True), loss_out.shape)


def tiles(src_rows, dst_rows, tile_src, tile_dst, tile_mask, tile_count):
    slots = tile_mask.shape[0]
    width = src_rows.shape[1]
    whole = lambda j, *_: (0, 0)
    return pl.pallas_call(
        functools.partial(tile_kernel, 0.5 * width ** -0.5),
        out_shape=(
            jax.ShapeDtypeStruct(src_rows.shape, BF16),
            jax.ShapeDtypeStruct(dst_rows.shape, BF16),
            jax.ShapeDtypeStruct((8, 128), F32),
        ),
        grid_spec=pltpu.PrefetchScalarGridSpec(
            num_scalar_prefetch=3,
            grid=(slots,),
            in_specs=[
                pl.BlockSpec(src_rows.shape, whole, pipeline_mode=pl.Buffered(1)),
                pl.BlockSpec(dst_rows.shape, whole, pipeline_mode=pl.Buffered(1)),
                pl.BlockSpec((1, BLOCK, BLOCK), lambda j, n, s, d: (jnp.minimum(j, n[0] - 1), 0, 0)),
            ],
            out_specs=[
                pl.BlockSpec(src_rows.shape, whole, pipeline_mode=pl.Buffered(1)),
                pl.BlockSpec(dst_rows.shape, whole, pipeline_mode=pl.Buffered(1)),
                pl.BlockSpec((8, 128), whole),
            ],
            scratch_shapes=[
                pltpu.VMEM(src_rows.shape, F32),
                pltpu.VMEM(dst_rows.shape, F32),
                pltpu.VMEM((BLOCK, BLOCK), BF16),
                pltpu.VMEM((8, BLOCK), F32),
                pltpu.VMEM((8, BLOCK), F32),
            ],
        ),
        compiler_params=pltpu.CompilerParams(vmem_limit_bytes=48 << 20),
        name="tiles",
    )(tile_count, tile_src, tile_dst, src_rows, dst_rows, tile_mask)


def advance(steps):
    return [step for step in steps if next(step, True) is None]


def together(*steps):
    steps = advance(steps)
    while steps:
        yield
        steps = advance(steps)


def finish(*steps):
    for _ in together(*steps):
        pass


def wavefront(steps):
    waiting = advance(steps)
    running = []
    while waiting or running:
        running = advance(waiting[:1] + running)
        waiting = waiting[1:]


def group(axis, n, inner):
    me = lax.axis_index(axis)
    return me, me // inner, lax.rem(me, inner)


def gather(axis, n, inner, src, place, send, recv):
    outer = n // inner
    me, at_o, at_i = group(axis, n, inner)

    def line(way, k):
        block = at_o - k if way == 0 else at_o + k
        ahead = me + inner if way == 0 else me - inner
        index = way * (outer - 1) + k
        return pltpu.make_async_remote_copy(
            src_ref=src if k == 0 else place(block * inner + at_i),
            dst_ref=place(me if k == 0 else block * inner + at_i),
            send_sem=send.at[index],
            recv_sem=recv.at[index],
            device_id={axis: ahead},
        )

    def sends(way, k):
        if way == 0:
            return jnp.logical_and(at_o - k >= 0, at_o < outer - 1)
        return jnp.logical_and(at_o + k < outer, at_o > 0)

    def arrived(way, k):
        block = at_o - 1 - k if way == 0 else at_o + 1 + k
        index = way * (outer - 1) + k
        here = place(block * inner + at_i)
        return pltpu.make_async_remote_copy(
            src_ref=here, dst_ref=here, send_sem=send.at[index], recv_sem=recv.at[index], device_id={axis: me}
        )

    def arrives(way, k):
        return at_o - 1 - k >= 0 if way == 0 else at_o + 1 + k < outer

    def across(j, block, slot, own, incoming=False):
        index = 2 * (outer - 1) + (j - 1) * (2 * outer - 1) + slot
        peer = at_o * inner + lax.rem(at_i + j, inner)
        where = place(block * inner + (lax.rem(at_i + inner - j, inner) if incoming else at_i))
        return pltpu.make_async_remote_copy(
            src_ref=src if own else where,
            dst_ref=where,
            send_sem=send.at[index],
            recv_sem=recv.at[index],
            device_id={axis: peer},
        )

    def slots():
        for way in range(2):
            for k in range(outer - 1):
                yield way, k, (at_o - 1 - k if way == 0 else at_o + 1 + k), 1 + way * (outer - 1) + k

    for way in range(2):
        @pl.when(sends(way, 0))
        def _(way=way):
            line(way, 0).start()
    for j in range(1, inner):
        across(j, at_o, 0, True).start()
    here = place(me)
    here[...] = src[...]
    yield
    for step in range(outer - 1):
        for way, k, block, slot in slots():
            if k != step:
                continue

            @pl.when(arrives(way, k))
            def _(way=way, k=k, block=block, slot=slot):
                arrived(way, k).wait_recv()
                for j in range(1, inner):
                    across(j, block, slot, False).start()
                if k + 1 < outer - 1:
                    @pl.when(sends(way, k + 1))
                    def _():
                        line(way, k + 1).start()
        yield
    for j in range(1, inner):
        across(j, at_o, 0, True, True).wait_recv()
        across(j, at_o, 0, True).wait_send()
    for way, k, block, slot in slots():
        @pl.when(arrives(way, k))
        def _(block=block, slot=slot):
            for j in range(1, inner):
                across(j, block, slot, False, True).wait_recv()
                across(j, block, slot, False).wait_send()

        @pl.when(sends(way, k))
        def _(way=way, k=k):
            line(way, k).wait_send()


def gather_sems(n, inner):
    outer = n // inner
    count = 2 * (outer - 1) + (inner - 1) * (2 * outer - 1)
    return [pltpu.SemaphoreType.DMA((count,)), pltpu.SemaphoreType.DMA((count,))]


def reduce(axis, n, inner, place, near, out, far, send, recv, result):
    outer = n // inner
    me, at_o, at_i = group(axis, n, inner)
    order = sorted(range(outer), key=lambda off: -min(off, outer - off))

    def across(j, off):
        index = (j - 1) * outer + off
        block = lax.rem(at_o + off, outer) * inner + lax.rem(at_i + j, inner)
        return pltpu.make_async_remote_copy(
            src_ref=place(block),
            dst_ref=near.at[index],
            send_sem=send.at[index],
            recv_sem=recv.at[index],
            device_id={axis: at_o * inner + lax.rem(at_i + j, inner)},
        )

    def along(off):
        index = (inner - 1) * outer + off - 1
        return pltpu.make_async_remote_copy(
            src_ref=out.at[off - 1],
            dst_ref=far.at[off - 1],
            send_sem=send.at[index],
            recv_sem=recv.at[index],
            device_id={axis: lax.rem(at_o + off, outer) * inner + at_i},
        )

    for off in order:
        for j in range(1, inner):
            across(j, off).start()
    yield
    for off in order:
        total = place(lax.rem(at_o + off, outer) * inner + at_i)[...].astype(F32)
        for j in range(1, inner):
            across(j, off).wait_recv()
            total = total + near[(j - 1) * outer + off].astype(F32)
        if off:
            out[off - 1] = total.astype(BF16)
            along(off).start()
    yield
    for off in order[:-1]:
        along(off).wait_recv()
        total = total + far[off - 1].astype(F32)
    result.append(total)
    for off in order:
        for j in range(1, inner):
            across(j, off).wait_send()
        if off:
            along(off).wait_send()


def reduce_scratch(n, inner, block):
    outer = n // inner
    count = (inner - 1) * outer + outer - 1
    return [
        pltpu.VMEM(((inner - 1) * outer,) + block, BF16),
        pltpu.VMEM((outer - 1,) + block, BF16),
        pltpu.VMEM((outer - 1,) + block, BF16),
        pltpu.SemaphoreType.DMA((count,)),
        pltpu.SemaphoreType.DMA((count,)),
    ]


def sum_over(axis, n, src, slots, send, recv, result):
    me = lax.axis_index(axis)

    def copy(j):
        return pltpu.make_async_remote_copy(
            src_ref=src,
            dst_ref=slots.at[j - 1],
            send_sem=send.at[j - 1],
            recv_sem=recv.at[j - 1],
            device_id={axis: lax.rem(me + j, n)},
        )

    for j in range(1, n):
        copy(j).start()
    yield
    total = src[...]
    for j in range(1, n):
        copy(j).wait_recv()
        total = total + slots[j - 1]
    result.append(total)
    for j in range(1, n):
        copy(j).wait_send()


def sum_scratch(n):
    return [
        pltpu.VMEM((n - 1, 8, 128), F32),
        pltpu.SemaphoreType.DMA((n - 1,)),
        pltpu.SemaphoreType.DMA((n - 1,)),
    ]


def greet(axes):
    barrier = pltpu.get_barrier_semaphore()
    total = 0
    for axis, n in axes:
        me = lax.axis_index(axis)
        for j in range(1, n):
            pl.semaphore_signal(barrier, inc=1, device_id={axis: lax.rem(me + j, n)})
        total += n - 1
    pl.semaphore_wait(barrier, total)


def rows_of(ref, size, part, chunk):
    return lambda block: ref.at[pl.ds(pl.multiple_of(block * size + chunk * part, part), part), :]


def units_of(ref, size, kind):
    return lambda block: ref.at[kind, pl.ds(pl.multiple_of(block * size, size), size), :]


def rows(ref, part, chunk):
    return ref.at[pl.ds(chunk * part, part), :]


def take(scratch, count):
    taken = scratch[:count]
    del scratch[:count]
    return taken


def gather_in_kernel(row, col, w_ref, x_ref, w_out, x_out, *scratch):
    greet((("row", row[0]), ("col", col[0])))
    scratch = list(scratch)
    kinds, units = w_ref.shape[:2]
    size = x_ref.shape[0]
    steps = [
        gather("col", *col, w_ref.at[kind], units_of(w_out, units, kind), *take(scratch, 2)) for kind in range(kinds)
    ]
    steps.append(gather("row", *row, x_ref, rows_of(x_out, size, size, 0), *take(scratch, 2)))
    finish(*steps)


def embed_kernel(row, col, chunks, branch_ref, x_ref, src_out, dst_out, held, *scratch):
    greet((("row", row[0]), ("col", col[0])))
    scratch = list(scratch)
    size = x_ref.shape[0]
    part = size // chunks

    def chain(chunk, sum_refs, col_sems, row_sems):
        branch = []
        yield from reduce("row", *row, rows_of(branch_ref, size, part, chunk), *sum_refs, branch)
        own = rows(held, part, chunk)
        own[...] = (rows(x_ref, part, chunk)[...].astype(F32) + branch[0]).astype(BF16)
        yield from together(
            gather("col", *col, own, rows_of(src_out, size, part, chunk), *col_sems),
            gather("row", *row, own, rows_of(dst_out, size, part, chunk), *row_sems),
        )

    wavefront([chain(chunk, take(scratch, 5), take(scratch, 2), take(scratch, 2)) for chunk in range(chunks)])


def grad_kernel(row, col, chunks, src_ref, dst_ref, tot_ref, grad_out, tot_out, held, tot_held, *scratch):
    greet((("row", row[0]), ("col", col[0])))
    scratch = list(scratch)
    size = held.shape[0]
    part = size // chunks

    def totals(row_refs, col_refs):
        first, second = [], []
        yield from sum_over("row", row[0], tot_ref, *row_refs, first)
        tot_held[...] = first[0]
        yield
        yield from sum_over("col", col[0], tot_held, *col_refs, second)
        tot_out[...] = second[0]

    def chain(chunk, col_refs, row_refs, row_sems):
        total = []
        yield from together(
            reduce("row", *row, rows_of(dst_ref, size, part, chunk), *row_refs, total),
            reduce("col", *col, rows_of(src_ref, size, part, chunk), *col_refs, total),
        )
        own = rows(held, part, chunk)
        own[...] = (total[0] + total[1]).astype(BF16)
        yield from gather("row", *row, own, rows_of(grad_out, size, part, chunk), *row_sems)

    steps = [totals(take(scratch, 3), take(scratch, 3))]
    steps += [chain(chunk, take(scratch, 5), take(scratch, 5), take(scratch, 2)) for chunk in range(chunks)]
    wavefront(steps)


def weight_kernel(col, part_ref, sum_out, *scratch):
    greet((("col", col[0]),))
    scratch = list(scratch)
    kinds, units = sum_out.shape[:2]

    def chain(kind, refs):
        total = []
        yield from reduce("col", *col, units_of(part_ref, units, kind), *refs, total)
        sum_out[kind] = total[0]

    wavefront([chain(kind, take(scratch, 5)) for kind in range(kinds)])


def remote(kernel, name, number, outs, scratch):
    vmem = pl.BlockSpec(memory_space=pltpu.VMEM)
    return pl.pallas_call(
        kernel,
        out_shape=outs,
        out_specs=jax.tree.map(lambda _: vmem, outs),
        scratch_shapes=scratch,
        compiler_params=pltpu.CompilerParams(
            collective_id=number, has_side_effects=True, vmem_limit_bytes=32 << 20
        ),
        name=name,
    )


def per_device(row, col, node_feats, w_gate, w_up, w_down, tile_src, tile_dst, tile_mask, tile_count):
    size, width = node_feats.shape
    units = w_down.shape[0]
    shaped = jax.ShapeDtypeStruct
    src_shape = shaped((col[0] * size, width), BF16)
    dst_shape = shaped((row[0] * size, width), BF16)
    stacked = jnp.stack((w_gate.T, w_up.T, w_down))
    weights, feats = remote(
        functools.partial(gather_in_kernel, row, col),
        "gather_in",
        0,
        (shaped((3, col[0] * units, width), BF16), dst_shape),
        gather_sems(*col) * 3 + gather_sems(*row),
    )(stacked, node_feats)
    gate_proj = dot_nt(feats, weights[0])
    up_proj = dot_nt(feats, weights[1])
    hidden = (jax.nn.silu(gate_proj) * up_proj).astype(BF16)
    branch = jnp.dot(hidden, weights[2], preferred_element_type=F32).astype(BF16)
    src_rows, dst_rows = remote(
        functools.partial(embed_kernel, row, col, CHUNKS),
        "embed",
        1,
        (src_shape, dst_shape),
        [pltpu.VMEM((size, width), BF16)]
        + (reduce_scratch(*row, (size // CHUNKS, width)) + gather_sems(*col) + gather_sems(*row)) * CHUNKS,
    )(branch, node_feats)
    src_part, dst_part, loss_part = tiles(src_rows, dst_rows, tile_src, tile_dst, tile_mask, tile_count)
    is_loss = lax.broadcasted_iota(jnp.int32, loss_part.shape, 0) == 0
    embed_grad, totals = remote(
        functools.partial(grad_kernel, row, col, CHUNKS),
        "grad",
        2,
        (dst_shape, shaped(loss_part.shape, F32)),
        [pltpu.VMEM((size, width), BF16), pltpu.VMEM(loss_part.shape, F32)]
        + sum_scratch(row[0]) + sum_scratch(col[0])
        + (
            reduce_scratch(*col, (size // CHUNKS, width))
            + reduce_scratch(*row, (size // CHUNKS, width))
            + gather_sems(*row)
        ) * CHUNKS,
    )(src_part, dst_part, jnp.where(is_loss, loss_part, tile_count[0].astype(F32)))
    hidden_grad = dot_nt(embed_grad, weights[2])
    sig = jax.nn.sigmoid(gate_proj)
    gate_grad = (hidden_grad * up_proj * sig * (1.0 + gate_proj * (1.0 - sig))).astype(BF16)
    up_grad = (hidden_grad * gate_proj * sig).astype(BF16)
    partial = jnp.stack(
        (dot_tn(gate_grad, feats).astype(BF16), dot_tn(up_grad, feats).astype(BF16), dot_tn(hidden, embed_grad).astype(BF16))
    )
    summed = remote(
        functools.partial(weight_kernel, col),
        "weight",
        3,
        shaped((3, units, width), F32),
        reduce_scratch(*col, (units, width)) * 3,
    )(partial)
    summed = summed * (0.5 * width ** -0.5 / totals[1, 0])
    entry_loss = totals[0, 0] / (totals[1, 0] * BLOCK * BLOCK)
    return (entry_loss, summed[0].T, summed[1].T, summed[2])


def solution(mesh):
    both = ("row", "col")
    in_specs = (
        P(both, None),
        P(None, both),
        P(None, both),
        P(both, None),
        P(both),
        P(both),
        P(both, None, None),
        P(both),
    )
    out_specs = (P(), P(None, both), P(None, both), P(both, None))
    row = (mesh.shape["row"], 2)
    col = (mesh.shape["col"], mesh.shape["col"] // 4)
    return jax.shard_map(functools.partial(per_device, row, col), mesh=mesh, in_specs=in_specs, out_specs=out_specs, check_vma=False)
```

```python
import functools
import math

import jax
import jax.numpy as jnp
from jax import lax
from jax.experimental import pallas as pl
from jax.experimental.pallas import tpu as pltpu
from jax.sharding import PartitionSpec as P

BLOCK = 512
CHUNKS = 4
F32 = jnp.float32
BF16 = jnp.bfloat16
NT = (((1,), (1,)), ((), ()))
TN = (((0,), (0,)), ((), ()))


def dot_nt(a, b):
    return lax.dot_general(a, b, NT, preferred_element_type=F32)


def dot_tn(a, b):
    return lax.dot_general(a, b, TN, preferred_element_type=F32)


def halve(x, op, rows):
    while x.shape[0] > rows:
        half = x.shape[0] // 2
        x = op(x[:half], x[half:])
    return x


def tile_kernel(half_scale, count_ref, src_id, dst_id, src_ref, dst_ref, mask_ref,
                src_out, dst_out, loss_out, src_acc, dst_acc, grad_buf, hinge_acc, log_acc):
    slot = pl.program_id(0)
    width = src_ref.shape[1]

    @pl.when(slot == 0)
    def _():
        src_acc[...] = jnp.zeros_like(src_acc)
        dst_acc[...] = jnp.zeros_like(dst_acc)
        hinge_acc[...] = jnp.zeros_like(hinge_acc)
        log_acc[...] = jnp.zeros_like(log_acc)

    @pl.when(slot < count_ref[0])
    def _():
        src_at = pl.ds(pl.multiple_of(src_id[slot] * BLOCK, BLOCK), BLOCK)
        dst_at = pl.ds(pl.multiple_of(dst_id[slot] * BLOCK, BLOCK), BLOCK)
        dst_block = dst_ref[dst_at, :]
        prods = None
        part = 128
        for lo in range(0, BLOCK, part):
            rows = pl.ds(pl.multiple_of(src_id[slot] * BLOCK + lo, part), part)
            raw = dot_nt(src_ref[rows, :], dst_block)
            sign = jnp.where(mask_ref[0, lo:lo + part, :] == 0, 1.0, -1.0)
            half = jnp.tanh(raw * half_scale)
            grad_buf[lo:lo + part, :] = (half + sign).astype(BF16)
            hinge_acc[...] += halve(jnp.maximum(raw * sign, 0.0), jnp.add, 8)
            prod = halve(1.0 + jnp.abs(half), jnp.multiply, 8)
            prods = prod if prods is None else prods * prod
        log_acc[...] += (BLOCK // 8) * math.log(2.0) - jnp.log(prods)
        grad = grad_buf[...]
        src_acc[src_at, :] += jnp.dot(grad, dst_block, preferred_element_type=F32)
        dst_acc[dst_at, :] += dot_tn(grad, src_ref[src_at, :])

    @pl.when(slot == pl.num_programs(0) - 1)
    def _():
        src_out[...] = src_acc[...].astype(BF16)
        dst_out[...] = dst_acc[...].astype(BF16)
        total = hinge_acc[...] * (2.0 * half_scale) + log_acc[...]
        loss_out[...] = jnp.broadcast_to(jnp.sum(total, keepdims=True), loss_out.shape)


def tiles(src_rows, dst_rows, tile_src, tile_dst, tile_mask, tile_count):
    slots = tile_mask.shape[0]
    width = src_rows.shape[1]
    whole = lambda j, *_: (0, 0)
    return pl.pallas_call(
        functools.partial(tile_kernel, 0.5 * width ** -0.5),
        out_shape=(
            jax.ShapeDtypeStruct(src_rows.shape, BF16),
            jax.ShapeDtypeStruct(dst_rows.shape, BF16),
            jax.ShapeDtypeStruct((8, 128), F32),
        ),
        grid_spec=pltpu.PrefetchScalarGridSpec(
            num_scalar_prefetch=3,
            grid=(slots,),
            in_specs=[
                pl.BlockSpec(src_rows.shape, whole, pipeline_mode=pl.Buffered(1)),
                pl.BlockSpec(dst_rows.shape, whole, pipeline_mode=pl.Buffered(1)),
                pl.BlockSpec((1, BLOCK, BLOCK), lambda j, n, s, d: (jnp.minimum(j, n[0] - 1), 0, 0)),
            ],
            out_specs=[
                pl.BlockSpec(src_rows.shape, whole, pipeline_mode=pl.Buffered(1)),
                pl.BlockSpec(dst_rows.shape, whole, pipeline_mode=pl.Buffered(1)),
                pl.BlockSpec((8, 128), whole),
            ],
            scratch_shapes=[
                pltpu.VMEM(src_rows.shape, F32),
                pltpu.VMEM(dst_rows.shape, F32),
                pltpu.VMEM((BLOCK, BLOCK), BF16),
                pltpu.VMEM((8, BLOCK), F32),
                pltpu.VMEM((8, BLOCK), F32),
            ],
        ),
        compiler_params=pltpu.CompilerParams(vmem_limit_bytes=48 << 20),
        name="tiles",
    )(tile_count, tile_src, tile_dst, src_rows, dst_rows, tile_mask)


def advance(steps):
    return [step for step in steps if next(step, True) is None]


def together(*steps):
    steps = advance(steps)
    while steps:
        yield
        steps = advance(steps)


def finish(*steps):
    for _ in together(*steps):
        pass


def wavefront(steps):
    waiting = advance(steps)
    running = []
    while waiting or running:
        running = advance(waiting[:1] + running)
        waiting = waiting[1:]


def group(axis, n, inner):
    me = lax.axis_index(axis)
    return me, me // inner, lax.rem(me, inner)


def gather(axis, n, inner, src, place, send, recv):
    outer = n // inner
    me, at_o, at_i = group(axis, n, inner)

    def line(way, k):
        block = at_o - k if way == 0 else at_o + k
        ahead = me + inner if way == 0 else me - inner
        index = way * (outer - 1) + k
        return pltpu.make_async_remote_copy(
            src_ref=src if k == 0 else place(block * inner + at_i),
            dst_ref=place(me if k == 0 else block * inner + at_i),
            send_sem=send.at[index],
            recv_sem=recv.at[index],
            device_id={axis: ahead},
        )

    def sends(way, k):
        if way == 0:
            return jnp.logical_and(at_o - k >= 0, at_o < outer - 1)
        return jnp.logical_and(at_o + k < outer, at_o > 0)

    def arrived(way, k):
        block = at_o - 1 - k if way == 0 else at_o + 1 + k
        index = way * (outer - 1) + k
        here = place(block * inner + at_i)
        return pltpu.make_async_remote_copy(
            src_ref=here, dst_ref=here, send_sem=send.at[index], recv_sem=recv.at[index], device_id={axis: me}
        )

    def arrives(way, k):
        return at_o - 1 - k >= 0 if way == 0 else at_o + 1 + k < outer

    def across(j, block, slot, own, incoming=False):
        index = 2 * (outer - 1) + (j - 1) * (2 * outer - 1) + slot
        peer = at_o * inner + lax.rem(at_i + j, inner)
        where = place(block * inner + (lax.rem(at_i + inner - j, inner) if incoming else at_i))
        return pltpu.make_async_remote_copy(
            src_ref=src if own else where,
            dst_ref=where,
            send_sem=send.at[index],
            recv_sem=recv.at[index],
            device_id={axis: peer},
        )

    def slots():
        for way in range(2):
            for k in range(outer - 1):
                yield way, k, (at_o - 1 - k if way == 0 else at_o + 1 + k), 1 + way * (outer - 1) + k

    for way in range(2):
        @pl.when(sends(way, 0))
        def _(way=way):
            line(way, 0).start()
    for j in range(1, inner):
        across(j, at_o, 0, True).start()
    here = place(me)
    here[...] = src[...]
    yield
    for step in range(outer - 1):
        for way, k, block, slot in slots():
            if k != step:
                continue

            @pl.when(arrives(way, k))
            def _(way=way, k=k, block=block, slot=slot):
                arrived(way, k).wait_recv()
                for j in range(1, inner):
                    across(j, block, slot, False).start()
                if k + 1 < outer - 1:
                    @pl.when(sends(way, k + 1))
                    def _():
                        line(way, k + 1).start()
        yield
    for j in range(1, inner):
        across(j, at_o, 0, True, True).wait_recv()
        across(j, at_o, 0, True).wait_send()
    for way, k, block, slot in slots():
        @pl.when(arrives(way, k))
        def _(block=block, slot=slot):
            for j in range(1, inner):
                across(j, block, slot, False, True).wait_recv()
                across(j, block, slot, False).wait_send()

        @pl.when(sends(way, k))
        def _(way=way, k=k):
            line(way, k).wait_send()


def gather_sems(n, inner):
    outer = n // inner
    count = 2 * (outer - 1) + (inner - 1) * (2 * outer - 1)
    return [pltpu.SemaphoreType.DMA((count,)), pltpu.SemaphoreType.DMA((count,))]


def reduce(axis, n, inner, place, near, out, far, send, recv, result, fine=False):
    outer = n // inner
    me, at_o, at_i = group(axis, n, inner)
    order = sorted(range(outer), key=lambda off: -min(off, outer - off))

    def across(j, off):
        index = (j - 1) * outer + off
        block = lax.rem(at_o + off, outer) * inner + lax.rem(at_i + j, inner)
        return pltpu.make_async_remote_copy(
            src_ref=place(block),
            dst_ref=near.at[index],
            send_sem=send.at[index],
            recv_sem=recv.at[index],
            device_id={axis: at_o * inner + lax.rem(at_i + j, inner)},
        )

    def along(off):
        index = (inner - 1) * outer + off - 1
        return pltpu.make_async_remote_copy(
            src_ref=out.at[off - 1],
            dst_ref=far.at[off - 1],
            send_sem=send.at[index],
            recv_sem=recv.at[index],
            device_id={axis: lax.rem(at_o + off, outer) * inner + at_i},
        )

    for off in order:
        for j in range(1, inner):
            across(j, off).start()
        if fine:
            yield
    if not fine:
        yield
    for off in order:
        total = place(lax.rem(at_o + off, outer) * inner + at_i)[...].astype(F32)
        for j in range(1, inner):
            across(j, off).wait_recv()
            total = total + near[(j - 1) * outer + off].astype(F32)
        if off:
            out[off - 1] = total.astype(BF16)
            along(off).start()
        if fine:
            yield
    if not fine:
        yield
    for off in order[:-1]:
        along(off).wait_recv()
        total = total + far[off - 1].astype(F32)
    result.append(total)
    for off in order:
        for j in range(1, inner):
            across(j, off).wait_send()
        if off:
            along(off).wait_send()


def reduce_scratch(n, inner, block):
    outer = n // inner
    count = (inner - 1) * outer + outer - 1
    return [
        pltpu.VMEM(((inner - 1) * outer,) + block, BF16),
        pltpu.VMEM((outer - 1,) + block, BF16),
        pltpu.VMEM((outer - 1,) + block, BF16),
        pltpu.SemaphoreType.DMA((count,)),
        pltpu.SemaphoreType.DMA((count,)),
    ]


def sum_over(axis, n, src, slots, send, recv, result):
    me = lax.axis_index(axis)

    def copy(j):
        return pltpu.make_async_remote_copy(
            src_ref=src,
            dst_ref=slots.at[j - 1],
            send_sem=send.at[j - 1],
            recv_sem=recv.at[j - 1],
            device_id={axis: lax.rem(me + j, n)},
        )

    for j in range(1, n):
        copy(j).start()
    yield
    total = src[...]
    for j in range(1, n):
        copy(j).wait_recv()
        total = total + slots[j - 1]
    result.append(total)
    for j in range(1, n):
        copy(j).wait_send()


def sum_scratch(n):
    return [
        pltpu.VMEM((n - 1, 8, 128), F32),
        pltpu.SemaphoreType.DMA((n - 1,)),
        pltpu.SemaphoreType.DMA((n - 1,)),
    ]


def greet(axes):
    barrier = pltpu.get_barrier_semaphore()
    total = 0
    for axis, n in axes:
        me = lax.axis_index(axis)
        for j in range(1, n):
            pl.semaphore_signal(barrier, inc=1, device_id={axis: lax.rem(me + j, n)})
        total += n - 1
    pl.semaphore_wait(barrier, total)


def rows_of(ref, size, part, chunk):
    return lambda block: ref.at[pl.ds(pl.multiple_of(block * size + chunk * part, part), part), :]


def units_of(ref, size, kind):
    return lambda block: ref.at[kind, pl.ds(pl.multiple_of(block * size, size), size), :]


def rows(ref, part, chunk):
    return ref.at[pl.ds(chunk * part, part), :]


def take(scratch, count):
    taken = scratch[:count]
    del scratch[:count]
    return taken


def gather_in_kernel(row, col, w_ref, x_ref, w_out, x_out, *scratch):
    greet((("row", row[0]), ("col", col[0])))
    scratch = list(scratch)
    kinds, units = w_ref.shape[:2]
    size = x_ref.shape[0]
    steps = [
        gather("col", *col, w_ref.at[kind], units_of(w_out, units, kind), *take(scratch, 2)) for kind in range(kinds)
    ]
    steps.append(gather("row", *row, x_ref, rows_of(x_out, size, size, 0), *take(scratch, 2)))
    finish(*steps)


def embed_kernel(row, col, chunks, branch_ref, x_ref, src_out, dst_out, held, *scratch):
    greet((("row", row[0]), ("col", col[0])))
    scratch = list(scratch)
    size = x_ref.shape[0]
    part = size // chunks

    def chain(chunk, sum_refs, col_sems, row_sems):
        branch = []
        yield from reduce("row", *row, rows_of(branch_ref, size, part, chunk), *sum_refs, branch)
        own = rows(held, part, chunk)
        own[...] = (rows(x_ref, part, chunk)[...].astype(F32) + branch[0]).astype(BF16)
        yield from together(
            gather("col", *col, own, rows_of(src_out, size, part, chunk), *col_sems),
            gather("row", *row, own, rows_of(dst_out, size, part, chunk), *row_sems),
        )

    wavefront([chain(chunk, take(scratch, 5), take(scratch, 2), take(scratch, 2)) for chunk in range(chunks)])


def grad_kernel(row, col, chunks, src_ref, dst_ref, tot_ref, grad_out, tot_out, held, tot_held, *scratch):
    greet((("row", row[0]), ("col", col[0])))
    scratch = list(scratch)
    size = held.shape[0]
    part = size // chunks

    def totals(row_refs, col_refs):
        first, second = [], []
        yield from sum_over("row", row[0], tot_ref, *row_refs, first)
        tot_held[...] = first[0]
        yield
        yield from sum_over("col", col[0], tot_held, *col_refs, second)
        tot_out[...] = second[0]

    def chain(chunk, col_refs, row_refs, row_sems):
        total = []
        yield from together(
            reduce("row", *row, rows_of(dst_ref, size, part, chunk), *row_refs, total),
            reduce("col", *col, rows_of(src_ref, size, part, chunk), *col_refs, total, True),
        )
        own = rows(held, part, chunk)
        own[...] = (total[0] + total[1]).astype(BF16)
        yield from gather("row", *row, own, rows_of(grad_out, size, part, chunk), *row_sems)

    steps = [totals(take(scratch, 3), take(scratch, 3))]
    steps += [chain(chunk, take(scratch, 5), take(scratch, 5), take(scratch, 2)) for chunk in range(chunks)]
    finish(*steps)


def weight_kernel(col, part_ref, sum_out, *scratch):
    greet((("col", col[0]),))
    scratch = list(scratch)
    kinds, units = sum_out.shape[:2]

    def chain(kind, refs):
        total = []
        yield from reduce("col", *col, units_of(part_ref, units, kind), *refs, total, True)
        sum_out[kind] = total[0]

    finish(*[chain(kind, take(scratch, 5)) for kind in range(kinds)])


def remote(kernel, name, number, outs, scratch):
    vmem = pl.BlockSpec(memory_space=pltpu.VMEM)
    return pl.pallas_call(
        kernel,
        out_shape=outs,
        out_specs=jax.tree.map(lambda _: vmem, outs),
        scratch_shapes=scratch,
        compiler_params=pltpu.CompilerParams(
            collective_id=number, has_side_effects=True, vmem_limit_bytes=32 << 20
        ),
        name=name,
    )


def per_device(row, col, node_feats, w_gate, w_up, w_down, tile_src, tile_dst, tile_mask, tile_count):
    size, width = node_feats.shape
    units = w_down.shape[0]
    shaped = jax.ShapeDtypeStruct
    src_shape = shaped((col[0] * size, width), BF16)
    dst_shape = shaped((row[0] * size, width), BF16)
    stacked = jnp.stack((w_gate.T, w_up.T, w_down))
    weights, feats = remote(
        functools.partial(gather_in_kernel, row, col),
        "gather_in",
        0,
        (shaped((3, col[0] * units, width), BF16), dst_shape),
        gather_sems(*col) * 3 + gather_sems(*row),
    )(stacked, node_feats)
    gate_proj = dot_nt(feats, weights[0])
    up_proj = dot_nt(feats, weights[1])
    hidden = (jax.nn.silu(gate_proj) * up_proj).astype(BF16)
    branch = jnp.dot(hidden, weights[2], preferred_element_type=F32).astype(BF16)
    src_rows, dst_rows = remote(
        functools.partial(embed_kernel, row, col, CHUNKS),
        "embed",
        1,
        (src_shape, dst_shape),
        [pltpu.VMEM((size, width), BF16)]
        + (reduce_scratch(*row, (size // CHUNKS, width)) + gather_sems(*col) + gather_sems(*row)) * CHUNKS,
    )(branch, node_feats)
    src_part, dst_part, loss_part = tiles(src_rows, dst_rows, tile_src, tile_dst, tile_mask, tile_count)
    is_loss = lax.broadcasted_iota(jnp.int32, loss_part.shape, 0) == 0
    embed_grad, totals = remote(
        functools.partial(grad_kernel, row, col, CHUNKS),
        "grad",
        2,
        (dst_shape, shaped(loss_part.shape, F32)),
        [pltpu.VMEM((size, width), BF16), pltpu.VMEM(loss_part.shape, F32)]
        + sum_scratch(row[0]) + sum_scratch(col[0])
        + (
            reduce_scratch(*col, (size // CHUNKS, width))
            + reduce_scratch(*row, (size // CHUNKS, width))
            + gather_sems(*row)
        ) * CHUNKS,
    )(src_part, dst_part, jnp.where(is_loss, loss_part, tile_count[0].astype(F32)))
    hidden_grad = dot_nt(embed_grad, weights[2])
    sig = jax.nn.sigmoid(gate_proj)
    gate_grad = (hidden_grad * up_proj * sig * (1.0 + gate_proj * (1.0 - sig))).astype(BF16)
    up_grad = (hidden_grad * gate_proj * sig).astype(BF16)
    partial = jnp.stack(
        (dot_tn(gate_grad, feats).astype(BF16), dot_tn(up_grad, feats).astype(BF16), dot_tn(hidden, embed_grad).astype(BF16))
    )
    summed = remote(
        functools.partial(weight_kernel, col),
        "weight",
        3,
        shaped((3, units, width), F32),
        reduce_scratch(*col, (units, width)) * 3,
    )(partial)
    summed = summed * (0.5 * width ** -0.5 / totals[1, 0])
    entry_loss = totals[0, 0] / (totals[1, 0] * BLOCK * BLOCK)
    return (entry_loss, summed[0].T, summed[1].T, summed[2])


def solution(mesh):
    both = ("row", "col")
    in_specs = (
        P(both, None),
        P(None, both),
        P(None, both),
        P(both, None),
        P(both),
        P(both),
        P(both, None, None),
        P(both),
    )
    out_specs = (P(), P(None, both), P(None, both), P(both, None))
    row = (mesh.shape["row"], 2)
    col = (mesh.shape["col"], mesh.shape["col"] // 4)
    return jax.shard_map(functools.partial(per_device, row, col), mesh=mesh, in_specs=in_specs, out_specs=out_specs, check_vma=False)
```

```python
import functools
import math

import jax
import jax.numpy as jnp
from jax import lax
from jax.experimental import pallas as pl
from jax.experimental.pallas import tpu as pltpu
from jax.sharding import PartitionSpec as P

BLOCK = 512
CHUNKS = 4
GRAD_CHUNKS = 2
F32 = jnp.float32
BF16 = jnp.bfloat16
NT = (((1,), (1,)), ((), ()))
TN = (((0,), (0,)), ((), ()))


def dot_nt(a, b):
    return lax.dot_general(a, b, NT, preferred_element_type=F32)


def dot_tn(a, b):
    return lax.dot_general(a, b, TN, preferred_element_type=F32)


def halve(x, op, rows):
    while x.shape[0] > rows:
        half = x.shape[0] // 2
        x = op(x[:half], x[half:])
    return x


def tile_kernel(half_scale, count_ref, src_id, dst_id, src_ref, dst_ref, mask_ref,
                src_out, dst_out, loss_out, src_acc, dst_acc, grad_buf, hinge_acc, log_acc):
    slot = pl.program_id(0)
    width = src_ref.shape[1]

    @pl.when(slot == 0)
    def _():
        src_acc[...] = jnp.zeros_like(src_acc)
        dst_acc[...] = jnp.zeros_like(dst_acc)
        hinge_acc[...] = jnp.zeros_like(hinge_acc)
        log_acc[...] = jnp.zeros_like(log_acc)

    @pl.when(slot < count_ref[0])
    def _():
        src_at = pl.ds(pl.multiple_of(src_id[slot] * BLOCK, BLOCK), BLOCK)
        dst_at = pl.ds(pl.multiple_of(dst_id[slot] * BLOCK, BLOCK), BLOCK)
        dst_block = dst_ref[dst_at, :]
        prods = None
        part = 128
        for lo in range(0, BLOCK, part):
            rows = pl.ds(pl.multiple_of(src_id[slot] * BLOCK + lo, part), part)
            raw = dot_nt(src_ref[rows, :], dst_block)
            sign = jnp.where(mask_ref[0, lo:lo + part, :] == 0, 1.0, -1.0)
            half = jnp.tanh(raw * half_scale)
            grad_buf[lo:lo + part, :] = (half + sign).astype(BF16)
            hinge_acc[...] += halve(jnp.maximum(raw * sign, 0.0), jnp.add, 8)
            prod = halve(1.0 + jnp.abs(half), jnp.multiply, 8)
            prods = prod if prods is None else prods * prod
        log_acc[...] += (BLOCK // 8) * math.log(2.0) - jnp.log(prods)
        grad = grad_buf[...]
        src_acc[src_at, :] += jnp.dot(grad, dst_block, preferred_element_type=F32)
        dst_acc[dst_at, :] += dot_tn(grad, src_ref[src_at, :])

    @pl.when(slot == pl.num_programs(0) - 1)
    def _():
        src_out[...] = src_acc[...].astype(BF16)
        dst_out[...] = dst_acc[...].astype(BF16)
        total = hinge_acc[...] * (2.0 * half_scale) + log_acc[...]
        loss_out[...] = jnp.broadcast_to(jnp.sum(total, keepdims=True), loss_out.shape)


def tiles(src_rows, dst_rows, tile_src, tile_dst, tile_mask, tile_count):
    slots = tile_mask.shape[0]
    width = src_rows.shape[1]
    whole = lambda j, *_: (0, 0)
    return pl.pallas_call(
        functools.partial(tile_kernel, 0.5 * width ** -0.5),
        out_shape=(
            jax.ShapeDtypeStruct(src_rows.shape, BF16),
            jax.ShapeDtypeStruct(dst_rows.shape, BF16),
            jax.ShapeDtypeStruct((8, 128), F32),
        ),
        grid_spec=pltpu.PrefetchScalarGridSpec(
            num_scalar_prefetch=3,
            grid=(slots,),
            in_specs=[
                pl.BlockSpec(src_rows.shape, whole, pipeline_mode=pl.Buffered(1)),
                pl.BlockSpec(dst_rows.shape, whole, pipeline_mode=pl.Buffered(1)),
                pl.BlockSpec((1, BLOCK, BLOCK), lambda j, n, s, d: (jnp.minimum(j, n[0] - 1), 0, 0)),
            ],
            out_specs=[
                pl.BlockSpec(src_rows.shape, whole, pipeline_mode=pl.Buffered(1)),
                pl.BlockSpec(dst_rows.shape, whole, pipeline_mode=pl.Buffered(1)),
                pl.BlockSpec((8, 128), whole),
            ],
            scratch_shapes=[
                pltpu.VMEM(src_rows.shape, F32),
                pltpu.VMEM(dst_rows.shape, F32),
                pltpu.VMEM((BLOCK, BLOCK), BF16),
                pltpu.VMEM((8, BLOCK), F32),
                pltpu.VMEM((8, BLOCK), F32),
            ],
        ),
        compiler_params=pltpu.CompilerParams(vmem_limit_bytes=48 << 20),
        name="tiles",
    )(tile_count, tile_src, tile_dst, src_rows, dst_rows, tile_mask)


def advance(steps):
    return [step for step in steps if next(step, True) is None]


def together(*steps):
    steps = advance(steps)
    while steps:
        yield
        steps = advance(steps)


def finish(*steps):
    for _ in together(*steps):
        pass


def wavefront(steps):
    waiting = advance(steps)
    running = []
    while waiting or running:
        running = advance(waiting[:1] + running)
        waiting = waiting[1:]


def group(axis, n, inner):
    me = lax.axis_index(axis)
    return me, me // inner, lax.rem(me, inner)


def gather(axis, n, inner, src, place, send, recv):
    outer = n // inner
    me, at_o, at_i = group(axis, n, inner)

    def line(way, k):
        block = at_o - k if way == 0 else at_o + k
        ahead = me + inner if way == 0 else me - inner
        index = way * (outer - 1) + k
        return pltpu.make_async_remote_copy(
            src_ref=src if k == 0 else place(block * inner + at_i),
            dst_ref=place(me if k == 0 else block * inner + at_i),
            send_sem=send.at[index],
            recv_sem=recv.at[index],
            device_id={axis: ahead},
        )

    def sends(way, k):
        if way == 0:
            return jnp.logical_and(at_o - k >= 0, at_o < outer - 1)
        return jnp.logical_and(at_o + k < outer, at_o > 0)

    def arrived(way, k):
        block = at_o - 1 - k if way == 0 else at_o + 1 + k
        index = way * (outer - 1) + k
        here = place(block * inner + at_i)
        return pltpu.make_async_remote_copy(
            src_ref=here, dst_ref=here, send_sem=send.at[index], recv_sem=recv.at[index], device_id={axis: me}
        )

    def arrives(way, k):
        return at_o - 1 - k >= 0 if way == 0 else at_o + 1 + k < outer

    def across(j, block, slot, own, incoming=False):
        index = 2 * (outer - 1) + (j - 1) * (2 * outer - 1) + slot
        peer = at_o * inner + lax.rem(at_i + j, inner)
        where = place(block * inner + (lax.rem(at_i + inner - j, inner) if incoming else at_i))
        return pltpu.make_async_remote_copy(
            src_ref=src if own else where,
            dst_ref=where,
            send_sem=send.at[index],
            recv_sem=recv.at[index],
            device_id={axis: peer},
        )

    def slots():
        for way in range(2):
            for k in range(outer - 1):
                yield way, k, (at_o - 1 - k if way == 0 else at_o + 1 + k), 1 + way * (outer - 1) + k

    for way in range(2):
        @pl.when(sends(way, 0))
        def _(way=way):
            line(way, 0).start()
    for j in range(1, inner):
        across(j, at_o, 0, True).start()
    here = place(me)
    here[...] = src[...]
    yield
    for step in range(outer - 1):
        for way, k, block, slot in slots():
            if k != step:
                continue

            @pl.when(arrives(way, k))
            def _(way=way, k=k, block=block, slot=slot):
                arrived(way, k).wait_recv()
                for j in range(1, inner):
                    across(j, block, slot, False).start()
                if k + 1 < outer - 1:
                    @pl.when(sends(way, k + 1))
                    def _():
                        line(way, k + 1).start()
        yield
    for j in range(1, inner):
        across(j, at_o, 0, True, True).wait_recv()
        across(j, at_o, 0, True).wait_send()
    for way, k, block, slot in slots():
        @pl.when(arrives(way, k))
        def _(block=block, slot=slot):
            for j in range(1, inner):
                across(j, block, slot, False, True).wait_recv()
                across(j, block, slot, False).wait_send()

        @pl.when(sends(way, k))
        def _(way=way, k=k):
            line(way, k).wait_send()


def gather_sems(n, inner):
    outer = n // inner
    count = 2 * (outer - 1) + (inner - 1) * (2 * outer - 1)
    return [pltpu.SemaphoreType.DMA((count,)), pltpu.SemaphoreType.DMA((count,))]


def reduce(axis, n, inner, place, near, out, far, send, recv, result, fine=False):
    outer = n // inner
    me, at_o, at_i = group(axis, n, inner)
    order = sorted(range(outer), key=lambda off: -min(off, outer - off))

    def across(j, off):
        index = (j - 1) * outer + off
        block = lax.rem(at_o + off, outer) * inner + lax.rem(at_i + j, inner)
        return pltpu.make_async_remote_copy(
            src_ref=place(block),
            dst_ref=near.at[index],
            send_sem=send.at[index],
            recv_sem=recv.at[index],
            device_id={axis: at_o * inner + lax.rem(at_i + j, inner)},
        )

    def along(off):
        index = (inner - 1) * outer + off - 1
        return pltpu.make_async_remote_copy(
            src_ref=out.at[off - 1],
            dst_ref=far.at[off - 1],
            send_sem=send.at[index],
            recv_sem=recv.at[index],
            device_id={axis: lax.rem(at_o + off, outer) * inner + at_i},
        )

    for off in order:
        for j in range(1, inner):
            across(j, off).start()
        if fine:
            yield
    if not fine:
        yield
    for off in order:
        total = place(lax.rem(at_o + off, outer) * inner + at_i)[...].astype(F32)
        for j in range(1, inner):
            across(j, off).wait_recv()
            total = total + near[(j - 1) * outer + off].astype(F32)
        if off:
            out[off - 1] = total.astype(BF16)
            along(off).start()
        if fine:
            yield
    if not fine:
        yield
    for off in order[:-1]:
        along(off).wait_recv()
        total = total + far[off - 1].astype(F32)
    result.append(total)
    for off in order:
        for j in range(1, inner):
            across(j, off).wait_send()
        if off:
            along(off).wait_send()


def reduce_scratch(n, inner, block):
    outer = n // inner
    count = (inner - 1) * outer + outer - 1
    return [
        pltpu.VMEM(((inner - 1) * outer,) + block, BF16),
        pltpu.VMEM((outer - 1,) + block, BF16),
        pltpu.VMEM((outer - 1,) + block, BF16),
        pltpu.SemaphoreType.DMA((count,)),
        pltpu.SemaphoreType.DMA((count,)),
    ]


def sum_over(axis, n, src, slots, send, recv, result):
    me = lax.axis_index(axis)

    def copy(j):
        return pltpu.make_async_remote_copy(
            src_ref=src,
            dst_ref=slots.at[j - 1],
            send_sem=send.at[j - 1],
            recv_sem=recv.at[j - 1],
            device_id={axis: lax.rem(me + j, n)},
        )

    for j in range(1, n):
        copy(j).start()
    yield
    total = src[...]
    for j in range(1, n):
        copy(j).wait_recv()
        total = total + slots[j - 1]
    result.append(total)
    for j in range(1, n):
        copy(j).wait_send()


def sum_scratch(n):
    return [
        pltpu.VMEM((n - 1, 8, 128), F32),
        pltpu.SemaphoreType.DMA((n - 1,)),
        pltpu.SemaphoreType.DMA((n - 1,)),
    ]


def greet(axes):
    barrier = pltpu.get_barrier_semaphore()
    total = 0
    for axis, n in axes:
        me = lax.axis_index(axis)
        for j in range(1, n):
            pl.semaphore_signal(barrier, inc=1, device_id={axis: lax.rem(me + j, n)})
        total += n - 1
    pl.semaphore_wait(barrier, total)


def rows_of(ref, size, part, chunk):
    return lambda block: ref.at[pl.ds(pl.multiple_of(block * size + chunk * part, part), part), :]


def units_of(ref, size, kind):
    return lambda block: ref.at[kind, pl.ds(pl.multiple_of(block * size, size), size), :]


def rows(ref, part, chunk):
    return ref.at[pl.ds(chunk * part, part), :]


def take(scratch, count):
    taken = scratch[:count]
    del scratch[:count]
    return taken


def gather_in_kernel(row, col, w_ref, x_ref, w_out, x_out, *scratch):
    greet((("row", row[0]), ("col", col[0])))
    scratch = list(scratch)
    kinds, units = w_ref.shape[:2]
    size = x_ref.shape[0]
    steps = [
        gather("col", *col, w_ref.at[kind], units_of(w_out, units, kind), *take(scratch, 2)) for kind in range(kinds)
    ]
    steps.append(gather("row", *row, x_ref, rows_of(x_out, size, size, 0), *take(scratch, 2)))
    finish(*steps)


def embed_kernel(row, col, chunks, branch_ref, x_ref, src_out, dst_out, held, *scratch):
    greet((("row", row[0]), ("col", col[0])))
    scratch = list(scratch)
    size = x_ref.shape[0]
    part = size // chunks

    def chain(chunk, sum_refs, col_sems, row_sems):
        branch = []
        yield from reduce("row", *row, rows_of(branch_ref, size, part, chunk), *sum_refs, branch)
        own = rows(held, part, chunk)
        own[...] = (rows(x_ref, part, chunk)[...].astype(F32) + branch[0]).astype(BF16)
        yield from together(
            gather("col", *col, own, rows_of(src_out, size, part, chunk), *col_sems),
            gather("row", *row, own, rows_of(dst_out, size, part, chunk), *row_sems),
        )

    wavefront([chain(chunk, take(scratch, 5), take(scratch, 2), take(scratch, 2)) for chunk in range(chunks)])


def grad_kernel(row, col, chunks, src_ref, dst_ref, tot_ref, grad_out, tot_out, held, tot_held, *scratch):
    greet((("row", row[0]), ("col", col[0])))
    scratch = list(scratch)
    size = held.shape[0]
    part = size // chunks

    def totals(row_refs, col_refs):
        first, second = [], []
        yield from sum_over("row", row[0], tot_ref, *row_refs, first)
        tot_held[...] = first[0]
        yield
        yield from sum_over("col", col[0], tot_held, *col_refs, second)
        tot_out[...] = second[0]

    def chain(chunk, col_refs, row_refs, row_sems):
        total = []
        yield from together(
            reduce("row", *row, rows_of(dst_ref, size, part, chunk), *row_refs, total),
            reduce("col", *col, rows_of(src_ref, size, part, chunk), *col_refs, total, True),
        )
        own = rows(held, part, chunk)
        own[...] = (total[0] + total[1]).astype(BF16)
        yield from gather("row", *row, own, rows_of(grad_out, size, part, chunk), *row_sems)

    steps = [totals(take(scratch, 3), take(scratch, 3))]
    steps += [chain(chunk, take(scratch, 5), take(scratch, 5), take(scratch, 2)) for chunk in range(chunks)]
    finish(*steps)


def weight_kernel(col, part_ref, sum_out, *scratch):
    greet((("col", col[0]),))
    scratch = list(scratch)
    kinds, units = sum_out.shape[:2]

    def chain(kind, refs):
        total = []
        yield from reduce("col", *col, units_of(part_ref, units, kind), *refs, total)
        sum_out[kind] = total[0]

    wavefront([chain(kind, take(scratch, 5)) for kind in range(kinds)])


def remote(kernel, name, number, outs, scratch):
    vmem = pl.BlockSpec(memory_space=pltpu.VMEM)
    return pl.pallas_call(
        kernel,
        out_shape=outs,
        out_specs=jax.tree.map(lambda _: vmem, outs),
        scratch_shapes=scratch,
        compiler_params=pltpu.CompilerParams(
            collective_id=number, has_side_effects=True, vmem_limit_bytes=32 << 20
        ),
        name=name,
    )


def per_device(row, col, node_feats, w_gate, w_up, w_down, tile_src, tile_dst, tile_mask, tile_count):
    size, width = node_feats.shape
    units = w_down.shape[0]
    shaped = jax.ShapeDtypeStruct
    src_shape = shaped((col[0] * size, width), BF16)
    dst_shape = shaped((row[0] * size, width), BF16)
    stacked = jnp.stack((w_gate.T, w_up.T, w_down))
    weights, feats = remote(
        functools.partial(gather_in_kernel, row, col),
        "gather_in",
        0,
        (shaped((3, col[0] * units, width), BF16), dst_shape),
        gather_sems(*col) * 3 + gather_sems(*row),
    )(stacked, node_feats)
    gate_proj = dot_nt(feats, weights[0])
    up_proj = dot_nt(feats, weights[1])
    hidden = (jax.nn.silu(gate_proj) * up_proj).astype(BF16)
    branch = jnp.dot(hidden, weights[2], preferred_element_type=F32).astype(BF16)
    src_rows, dst_rows = remote(
        functools.partial(embed_kernel, row, col, CHUNKS),
        "embed",
        1,
        (src_shape, dst_shape),
        [pltpu.VMEM((size, width), BF16)]
        + (reduce_scratch(*row, (size // CHUNKS, width)) + gather_sems(*col) + gather_sems(*row)) * CHUNKS,
    )(branch, node_feats)
    src_part, dst_part, loss_part = tiles(src_rows, dst_rows, tile_src, tile_dst, tile_mask, tile_count)
    is_loss = lax.broadcasted_iota(jnp.int32, loss_part.shape, 0) == 0
    embed_grad, totals = remote(
        functools.partial(grad_kernel, row, col, GRAD_CHUNKS),
        "grad",
        2,
        (dst_shape, shaped(loss_part.shape, F32)),
        [pltpu.VMEM((size, width), BF16), pltpu.VMEM(loss_part.shape, F32)]
        + sum_scratch(row[0]) + sum_scratch(col[0])
        + (
            reduce_scratch(*col, (size // GRAD_CHUNKS, width))
            + reduce_scratch(*row, (size // GRAD_CHUNKS, width))
            + gather_sems(*row)
        ) * GRAD_CHUNKS,
    )(src_part, dst_part, jnp.where(is_loss, loss_part, tile_count[0].astype(F32)))
    hidden_grad = dot_nt(embed_grad, weights[2])
    sig = jax.nn.sigmoid(gate_proj)
    gate_grad = (hidden_grad * up_proj * sig * (1.0 + gate_proj * (1.0 - sig))).astype(BF16)
    up_grad = (hidden_grad * gate_proj * sig).astype(BF16)
    partial = jnp.stack(
        (dot_tn(gate_grad, feats).astype(BF16), dot_tn(up_grad, feats).astype(BF16), dot_tn(hidden, embed_grad).astype(BF16))
    )
    summed = remote(
        functools.partial(weight_kernel, col),
        "weight",
        3,
        shaped((3, units, width), F32),
        reduce_scratch(*col, (units, width)) * 3,
    )(partial)
    summed = summed * (0.5 * width ** -0.5 / totals[1, 0])
    entry_loss = totals[0, 0] / (totals[1, 0] * BLOCK * BLOCK)
    return (entry_loss, summed[0].T, summed[1].T, summed[2])


def solution(mesh):
    both = ("row", "col")
    in_specs = (
        P(both, None),
        P(None, both),
        P(None, both),
        P(both, None),
        P(both),
        P(both),
        P(both, None, None),
        P(both),
    )
    out_specs = (P(), P(None, both), P(None, both), P(both, None))
    row = (mesh.shape["row"], 2)
    col = (mesh.shape["col"], mesh.shape["col"] // 4)
    return jax.shard_map(functools.partial(per_device, row, col), mesh=mesh, in_specs=in_specs, out_specs=out_specs, check_vma=False)
```
